128 devices in a mesh: traj: 4 (over y_lo, core), grid: 32 (over z, x, y_hi).
Axes of the slice: x: 4, y: 4 (y_hi: 2, y_lo: 2; y = y_hi * 2 + y_lo), z: 4, core: 2. Of those that a mesh axis runs over, the one named last changes fastest.
Arguments:
- state: bfloat16 [16, 24, 640, 1280], P('traj', None, 'grid'), may hold values from -6 to 6
- counts: int32 [16], replicated, may hold values from 0 to 4, as said below
- slot_perm: int32 [16], replicated, may hold values from 0 to 15, each once
- legendre: bfloat16 [640, 2, 320, 320], P(('traj', 'grid')), may hold values from -0.3125 to 0.3125
- quad_weight: float32 [320], replicated, may hold values from 0.5 to 1.5
- diffusion: float32 [24], replicated, may hold values from 0.5 to 20
Outputs:
- smoothed: bfloat16 [16, 24, 640, 1280], P('traj', None, 'grid')
The draws below stay inside these ranges and needn't reach their ends.
Inputs may be any that keep to these rules, and one draw needn't show every extreme that they name: Offspring counts of the 16 trajectories; they sum to 16, at least one trajectory has 4 copies, and at least one has none. `slot_perm`: each of the 16 slots appears once.
All inputs are finite; a program needn't handle non-finite values.
Results may differ from the reference program's by a relative error of at most 0.0077.
Values may be sent and summed in bfloat16 or wider, within the bound.
A program may use at most 192 MiB of HBM per device.

```python
import math
import jax
import jax.numpy as jnp
from jax import lax

NLAT = 640
NLON = 1280
NM = 640
HALF = 320
FL = 24
TRAJ = 16


def draw_counts(key, part):
    key_one, key_two = jax.random.split(key, 2)
    most_copies = TRAJ // 4
    others = TRAJ - 1
    relabel = jax.random.permutation(key_one, TRAJ).astype(jnp.int32)
    seat_order = jax.random.permutation(key_two, others * most_copies).astype(jnp.int32)
    rest_owner = 1 + seat_order[:TRAJ - most_copies] // most_copies
    owner_rank = jnp.concatenate([jnp.zeros((most_copies,), jnp.int32), rest_owner.astype(jnp.int32)])
    owners = jnp.take(relabel, owner_rank)
    members = jnp.arange(TRAJ, dtype=jnp.int32)
    return jnp.sum((owners[:, None] == members[None, :]).astype(jnp.int32), axis=0).astype(jnp.int32)


def shard_levels(own_key, dims, shards, smallest, high):
    gain = 1.0
    for dim, blocks in shards:
        heights = jax.random.uniform(jax.random.fold_in(jax.random.fold_in(own_key, 6), dim), (blocks,), jnp.float32, smallest / len(shards), high / len(shards))
        gain = gain * jnp.repeat(jnp.exp(heights), dims[dim] // blocks).reshape((-1,) + (1,) * (len(dims) - 1 - dim))
    return gain


def gaussian(key, dims, scale, bound, pieces=(), held_as=jnp.bfloat16):
    gain = shard_levels(key, dims, pieces, -0.22, 0.18) if pieces else 1.0
    drawn = jax.random.normal(key, dims, jnp.float32) * scale * gain
    return jnp.minimum(jnp.maximum(drawn, -bound), bound).astype(held_as)


def setup_inputs(seed: int = 0) -> dict:
    arg_keys = jax.random.split(jax.random.key(seed), 7)
    state = gaussian(arg_keys[0], (TRAJ, FL, NLAT, NLON), 1.0, 6.0, ((0, 4), (2, 32)))
    counts = draw_counts(jax.random.fold_in(arg_keys[6], 71), 0)
    slot_perm = jax.random.permutation(arg_keys[2], TRAJ).astype(jnp.int32)
    legendre = gaussian(arg_keys[3], (NM, 2, HALF, HALF), HALF ** -0.5, 0.3125, ((0, 128),))
    quad_weight = jnp.clip(jax.random.uniform(arg_keys[4], (HALF,), jnp.float32, 0.5, 1.5), 0.5, 1.5)
    diffusion = jnp.clip(jnp.exp(jax.random.uniform(arg_keys[5], (FL,), jnp.float32, math.log(0.5), math.log(20.0))), 0.5, 20.0)
    return {"state": state, "counts": counts, "slot_perm": slot_perm, "legendre": legendre, "quad_weight": quad_weight, "diffusion": diffusion}


def parent_slots(counts, slot_perm):
    member_count = counts.shape[0]
    position = jnp.arange(member_count, dtype=jnp.int32)
    copy_end = jnp.cumsum(counts).astype(jnp.int32)
    copy_parent = jnp.sum((copy_end[None, :] <= position[:, None]).astype(jnp.int32), axis=1).astype(jnp.int32)
    landing = (slot_perm[:, None] == position[None, :]).astype(jnp.int32)
    return jnp.sum(landing * copy_parent[:, None], axis=0).astype(jnp.int32)


def trig_pair(wave_order, lon_count):
    lon_points = jnp.arange(lon_count, dtype=jnp.int32)
    phase_angle = ((wave_order[:, None] * lon_points[None, :]) % lon_count).astype(jnp.float32) * (2.0 * math.pi / lon_count)
    return jnp.stack([jnp.cos(phase_angle), -jnp.sin(phase_angle)], axis=1)


def forward_table(wave_order, lon_count):
    return (trig_pair(wave_order, lon_count) / lon_count).astype(jnp.bfloat16)


def inverse_table(wave_order, lon_count):
    doubled = jnp.where(wave_order == 0, 1.0, 2.0).astype(jnp.float32)
    return (trig_pair(wave_order, lon_count) * doubled[:, None, None]).astype(jnp.bfloat16)


def spectral_filter(wave_rows, legendre_wide, wave_ids, quad_weight, diffusion):
    wave_here, halves, members, levels, lat_count = wave_rows.shape
    hemisphere = lat_count // 2
    north_rows = wave_rows[..., :hemisphere].astype(jnp.float32)
    south_rows = jnp.flip(wave_rows[..., hemisphere:], axis=-1).astype(jnp.float32)
    even_sum = ((north_rows + south_rows) * quad_weight).astype(jnp.bfloat16)
    odd_diff = ((north_rows - south_rows) * quad_weight).astype(jnp.bfloat16)
    paired = jnp.stack([even_sum, odd_diff], axis=1).reshape(wave_here, 2, halves * members * levels, hemisphere)
    spectrum = jnp.einsum("mpkl,mpcl->mpkc", legendre_wide, paired.astype(jnp.float32))
    parity = jnp.arange(2, dtype=jnp.int32)
    degree = 2 * jnp.arange(hemisphere, dtype=jnp.int32)[None, None, :] + (wave_ids[:, None, None] + parity[None, :, None]) % 2
    degree_ratio = (degree * (degree + 1)).astype(jnp.float32) / float(lat_count * (lat_count - 1))
    rate_cols = jnp.broadcast_to(diffusion, (halves, members, levels)).reshape(-1)
    damping = 1.0 / (1.0 + rate_cols[None, None, None, :] * (degree_ratio * degree_ratio)[..., None])
    retained = (degree >= wave_ids[:, None, None])[..., None]
    filtered = jnp.where(retained, spectrum * damping, 0.0).astype(jnp.bfloat16)
    returned = jnp.einsum("mpkl,mpkc->mpcl", legendre_wide, filtered.astype(jnp.float32))
    north_out = returned[:, 0] + returned[:, 1]
    south_out = returned[:, 0] - returned[:, 1]
    lat_rows = jnp.concatenate([north_out, jnp.flip(south_out, axis=-1)], axis=-1)
    return lat_rows.astype(jnp.bfloat16).reshape(wave_here, halves, members, levels, lat_count)


def reference(state, counts, slot_perm, legendre, quad_weight, diffusion):
    parents = parent_slots(counts, slot_perm)
    wave_ids = jnp.arange(NM, dtype=jnp.int32)
    forward_wide = forward_table(wave_ids, NLON).astype(jnp.float32)
    inverse_wide = inverse_table(wave_ids, NLON).astype(jnp.float32)
    legendre_wide = legendre.astype(jnp.float32)

    def one_member(parent):
        member = lax.dynamic_index_in_dim(state, parent, 0, keepdims=False).astype(jnp.float32)
        fourier = jnp.einsum("flj,mrj->mrfl", member, forward_wide).astype(jnp.bfloat16)
        waves_out = spectral_filter(fourier[:, :, None], legendre_wide, wave_ids, quad_weight, diffusion)
        smoothed = jnp.einsum("mrtfl,mrj->tflj", waves_out.astype(jnp.float32), inverse_wide)
        return smoothed[0].astype(jnp.bfloat16)

    return lax.map(one_member, parents)
```

```python
import functools
import math

import jax
import jax.numpy as jnp
import numpy as np
from jax import lax
from jax.experimental import pallas as pl
from jax.experimental.pallas import tpu as pltpu
from jax.sharding import PartitionSpec as P

MESH = pl.DeviceIdType.MESH
LANES = 128
MAIN = 96
TAIL = 32
BIG = 60 * 2**20


def angle_tables(lon_count):
    points = np.arange(lon_count)
    coarse = (32 * np.arange(lon_count // 64)[:, None] * points[None, :]) % lon_count
    fine = (np.arange(32)[:, None] * points[None, :]) % lon_count
    unit = 2.0 * math.pi / lon_count
    fine_angle = (fine[:, None, :] * unit + np.arange(2)[None, :, None] * (math.pi / 2)).reshape(64, lon_count)
    coarse_angle = (coarse * unit)[:, None, :]
    return [np.asarray(t, np.float32) for t in (np.cos(coarse_angle), np.sin(coarse_angle), np.cos(fine_angle), np.sin(fine_angle))]


def fill_table(table, coarse_cos, coarse_sin, fine_cos, fine_sin, scale, halve_first):
    @pl.loop(0, coarse_cos.shape[0])
    def _(a):
        rows = (coarse_cos[a] * scale) * fine_cos[...] - (coarse_sin[a] * scale) * fine_sin[...]
        if halve_first:
            row = lax.broadcasted_iota(jnp.int32, rows.shape, 0)
            rows = jnp.where(jnp.logical_and(a == 0, row < 2), rows * 0.5, rows)
        table[pl.ds(pl.multiple_of(a * 64, 64), 64), :] = rows.astype(table.dtype)


def forward_kernel(x_ref, cc, cs, fc, fs, y_ref, table):
    @pl.when(pl.program_id(0) == 0)
    def _():
        fill_table(table, cc, cs, fc, fs, 1.0 / x_ref.shape[-1], False)

    tail = jnp.concatenate([x_ref[t, 0, 3].astype(jnp.float32) for t in range(4)], axis=0)
    tiles = []
    for a in range(3):
        tiles += [x_ref[t, 0, a].astype(jnp.float32) for t in range(4)]
        tiles.append(tail[TAIL * a:TAIL * (a + 1)])
    rows = jnp.concatenate(tiles, axis=0).astype(jnp.bfloat16)
    waves = lax.dot_general(table[...], rows, (((1,), (1,)), ((), ())), preferred_element_type=jnp.float32)
    for a in range(3):
        y_ref[a] = waves[:, LANES * a:LANES * (a + 1)].astype(jnp.bfloat16)


def inverse_kernel(z_ref, cc, cs, fc, fs, x_ref, table):
    @pl.when(pl.program_id(0) == 0)
    def _():
        fill_table(table, cc, cs, fc, fs, 2.0, True)

    waves = jnp.concatenate([z_ref[a] for a in range(3)], axis=1)
    rows = lax.dot_general(waves, table[...], (((0,), (0,)), ((), ())), preferred_element_type=jnp.float32)
    for a in range(3):
        for t in range(4):
            base = LANES * a + 24 * t
            x_ref[t, 0, a] = rows[base:base + 24].astype(jnp.bfloat16)
    tail = jnp.concatenate([rows[LANES * a + MAIN:LANES * (a + 1)] for a in range(3)], axis=0)
    for t in range(4):
        x_ref[t, 0, 3] = tail[24 * t:24 * t + 24].astype(jnp.bfloat16)


def table_specs(lon_count):
    return [
        pl.BlockSpec((lon_count // 64, 1, lon_count), lambda q: (0, 0, 0)),
        pl.BlockSpec((lon_count // 64, 1, lon_count), lambda q: (0, 0, 0)),
        pl.BlockSpec((64, lon_count), lambda q: (0, 0)),
        pl.BlockSpec((64, lon_count), lambda q: (0, 0)),
    ]


def forward_waves(rows, tables):
    lon_count = rows.shape[-1]
    return pl.pallas_call(
        forward_kernel,
        grid=(5,),
        out_shape=jax.ShapeDtypeStruct((15, lon_count, LANES), jnp.bfloat16),
        in_specs=[pl.BlockSpec((4, 1, 4, 24, lon_count), lambda q: (0, q, 0, 0, 0))] + table_specs(lon_count),
        out_specs=pl.BlockSpec((3, lon_count, LANES), lambda q: (q, 0, 0)),
        scratch_shapes=[pltpu.VMEM((lon_count, lon_count), jnp.bfloat16)],
        compiler_params=pltpu.CompilerParams(vmem_limit_bytes=BIG),
    )(rows, *tables)


def inverse_waves(waves, tables):
    lon_count = waves.shape[1]
    return pl.pallas_call(
        inverse_kernel,
        grid=(5,),
        out_shape=jax.ShapeDtypeStruct((4, 5, 4, 24, lon_count), jnp.bfloat16),
        in_specs=[pl.BlockSpec((3, lon_count, LANES), lambda q: (q, 0, 0))] + table_specs(lon_count),
        out_specs=pl.BlockSpec((4, 1, 4, 24, lon_count), lambda q: (0, q, 0, 0, 0)),
        scratch_shapes=[pltpu.VMEM((lon_count, lon_count), jnp.bfloat16)],
        compiler_params=pltpu.CompilerParams(vmem_limit_bytes=BIG),
    )(waves, *tables)


def partner(step):
    traj, grid = lax.axis_index("traj"), lax.axis_index("grid")
    core = (traj % 2 + step % 2) % 2
    y = (grid % 2 * 2 + traj // 2 + step // 2 % 4) % 4
    x = (grid // 2 % 4 + step // 8 % 4) % 4
    z = (grid // 8 + step // 32) % 4
    return y % 2 * 2 + core, (z * 4 + x) * 2 + y // 2


def slab_slot(grid):
    return jnp.where(grid < 16, grid, 47 - grid)


def greet():
    barrier = pltpu.get_barrier_semaphore()

    def signal(step, carry):
        pl.semaphore_signal(barrier, inc=1, device_id=partner(step), device_id_type=MESH)
        return carry

    lax.fori_loop(1, 128, signal, 0)
    pl.semaphore_wait(barrier, 127)


def exchange(source, target, send_sem, recv_sem, local_sem):
    traj, grid = lax.axis_index("traj"), lax.axis_index("grid")
    own = pltpu.make_async_copy(source(traj, grid), target(traj, grid), local_sem)
    own.start()
    greet()

    def copy_to(step):
        there = partner(step)
        return pltpu.make_async_remote_copy(
            source(*there), target(traj, grid), send_sem.at[step], recv_sem.at[step],
            device_id=there, device_id_type=MESH,
        )

    def send(index, carry):
        copy_to(index * 37 % 128).start()
        return carry

    def finish(step, carry):
        copy_to(step).wait()
        return carry

    lax.fori_loop(1, 128, send, 0)
    lax.fori_loop(1, 128, finish, 0)
    own.wait()


def to_owner_kernel(y_ref, r_ref, send_sem, recv_sem, local_sem):
    exchange(
        lambda traj, grid: y_ref.at[:, traj * 32 + grid],
        lambda traj, grid: r_ref.at[traj, :, :, slab_slot(grid)],
        send_sem, recv_sem, local_sem,
    )


def to_slab_kernel(w_ref, z_ref, send_sem, recv_sem, local_sem):
    exchange(
        lambda traj, grid: w_ref.at[traj, :, :, slab_slot(grid)],
        lambda traj, grid: z_ref.at[:, traj * 32 + grid],
        send_sem, recv_sem, local_sem,
    )


def exchange_call(kernel, operand, shape, collective_id):
    return pl.pallas_call(
        kernel,
        out_shape=jax.ShapeDtypeStruct(shape, jnp.bfloat16),
        in_specs=[pl.BlockSpec(memory_space=pl.ANY)],
        out_specs=pl.BlockSpec(memory_space=pl.ANY),
        scratch_shapes=[pltpu.SemaphoreType.DMA((128,)), pltpu.SemaphoreType.DMA((128,)), pltpu.SemaphoreType.DMA],
        compiler_params=pltpu.CompilerParams(collective_id=collective_id, has_side_effects=True),
    )(operand)


def spectral_kernel(first_ref, r_ref, leg_ref, weight_ref, rate_ref, order_ref, pick_ref, w_ref, split, paired, cloned, woven):
    wave = first_ref[0] + pl.program_id(0)
    lane = lax.broadcasted_iota(jnp.int32, (64, LANES), 1)

    @pl.loop(0, 4)
    def _(g):
        for q in range(5):
            parts = [r_ref[g, 3 * q + a, 0].astype(jnp.float32) for a in range(3)]
            moved = [pltpu.roll(parts[a], TAIL * (a + 1), 1) for a in range(3)]
            parts.append(jnp.where(lane < TAIL, moved[0], jnp.where(lane < 2 * TAIL, moved[1], moved[2])))
            for i in range(4):
                split[4 * q + i] = parts[i]
        for q in range(5):
            for i in range(4):
                rows = slice(80 * i + 16 * q, 80 * i + 16 * q + 16)
                weight = weight_ref[rows]
                for r in range(2):
                    north = split[4 * q + i, pl.ds(r, 16, stride=2), :]
                    south = split[4 * (4 - q) + 3 - i, pl.ds(32 + r, 16, stride=2), :]
                    paired[0, 4 * r + g, rows] = ((north + south) * weight).astype(jnp.bfloat16)
                    paired[1, 4 * r + g, rows] = ((north - south) * weight).astype(jnp.bfloat16)

    half = leg_ref.shape[-1]
    take = (lax.broadcasted_iota(jnp.int32, (half, half), 0) == order_ref[...]).astype(jnp.bfloat16)
    returned = []
    for p in range(2):
        table = jnp.dot(leg_ref[0, p], take, preferred_element_type=jnp.float32).astype(jnp.bfloat16)
        columns = jnp.concatenate([paired[p, c] for c in range(8)], axis=1)
        spectrum = jnp.dot(table, columns, preferred_element_type=jnp.float32)
        degree = 2 * lax.broadcasted_iota(jnp.int32, (half, LANES), 0) + (wave + p) % 2
        ratio = (degree * (degree + 1)).astype(jnp.float32) / float(2 * half * (2 * half - 1))
        damping = 1.0 / (1.0 + rate_ref[...] * (ratio * ratio))
        keep = degree >= wave
        for r in range(2):
            kept = [
                jnp.where(keep, spectrum[:, LANES * c:LANES * (c + 1)] * damping, 0.0).astype(jnp.bfloat16)
                for c in range(4 * r, 4 * r + 4)
            ]
            cloned[p, :, 512 * r:512 * (r + 1)] = jnp.dot(
                jnp.concatenate(kept, axis=1), pick_ref[...], preferred_element_type=jnp.float32
            ).astype(jnp.bfloat16)
        returned.append(
            lax.dot_general(table, cloned[p], (((0,), (0,)), ((), ())), preferred_element_type=jnp.float32)
        )
    main_lanes = lax.broadcasted_iota(jnp.int32, (80, LANES), 1) < MAIN
    for c in range(8):
        r, g = c // 4, c % 4
        cols = slice(LANES * c, LANES * (c + 1))
        even, odd = returned[0][:, cols], returned[1][:, cols]
        north, south = even + odd, even - odd
        for a in range(3):
            shift = MAIN - TAIL * a
            upper = jnp.where(main_lanes, north[80 * a:80 * a + 80], pltpu.roll(north[240:320], shift, 1))
            lower = jnp.where(main_lanes, south[80 * (3 - a):80 * (3 - a) + 80], pltpu.roll(south[0:80], shift, 1))
            for q in range(5):
                woven[15 * g + 3 * q + a, pl.ds(r, 16, stride=2), :] = upper[16 * q:16 * q + 16]
                woven[15 * g + 3 * q + a, pl.ds(32 + r, 16, stride=2), :] = lower[16 * (4 - q):16 * (4 - q) + 16]
    for g in range(4):
        for tile in range(15):
            w_ref[g, tile, 0] = woven[15 * g + tile].astype(jnp.bfloat16)


def spectral_filter(first, received, legendre, weight, rate, order, pick):
    waves, _, half, _ = legendre.shape
    block = pl.BlockSpec((4, 15, 1, 64, LANES), lambda m: (0, 0, m, 0, 0))
    return pl.pallas_call(
        spectral_kernel,
        grid=(waves,),
        out_shape=jax.ShapeDtypeStruct(received.shape, jnp.bfloat16),
        in_specs=[
            pl.BlockSpec(memory_space=pltpu.SMEM),
            block,
            pl.BlockSpec((1, 2, half, half), lambda m: (m, 0, 0, 0)),
            pl.BlockSpec((half, 1), lambda m: (0, 0)),
            pl.BlockSpec((1, LANES), lambda m: (0, 0)),
            pl.BlockSpec((1, half), lambda m: (0, 0)),
            pl.BlockSpec((4 * LANES, 4 * LANES), lambda m: (0, 0)),
        ],
        out_specs=block,
        scratch_shapes=[
            pltpu.VMEM((20, 64, LANES), jnp.float32),
            pltpu.VMEM((2, 8, half, LANES), jnp.bfloat16),
            pltpu.VMEM((2, half, 8 * LANES), jnp.bfloat16),
            pltpu.VMEM((60, 64, LANES), jnp.float32),
        ],
        compiler_params=pltpu.CompilerParams(vmem_limit_bytes=BIG),
    )(first, received, legendre, weight, rate, order, pick)


def parent_slots(counts, slot_perm):
    member_count = counts.shape[0]
    position = jnp.arange(member_count, dtype=jnp.int32)
    copy_end = jnp.sum(jnp.where(position[None, :] <= position[:, None], counts[None, :], 0), axis=1)
    copy_parent = jnp.sum((copy_end[None, :] <= position[:, None]).astype(jnp.int32), axis=1)
    landing = (slot_perm[:, None] == position[None, :]).astype(jnp.int32)
    return jnp.sum(landing * copy_parent[:, None], axis=0)


def clone_columns(parents):
    column = np.arange(4 * LANES)
    member = np.where(column % LANES < MAIN, column // LANES * 4 + column % LANES // 24, -1)
    field = column % LANES % 24
    slot = (member[None, :] == np.arange(16)[:, None])
    wanted = jnp.sum(jnp.where(slot, parents[:, None], 0), axis=0)
    same = (member[:, None] == wanted[None, :]) & (field[:, None] == field[None, :]) & (member >= 0)[None, :]
    return same.astype(jnp.bfloat16)


def on_device(state, counts, slot_perm, legendre, quad_weight, diffusion):
    lon_count = state.shape[-1]
    own_waves = legendre.shape[0]
    half = legendre.shape[-1]
    tables = angle_tables(lon_count)
    device = lax.axis_index("traj") * 32 + lax.axis_index("grid")
    pick = clone_columns(parent_slots(counts, slot_perm))
    first = (device * own_waves).astype(jnp.int32)[None]
    weight = quad_weight.reshape(16, 5, 4).transpose(2, 1, 0).reshape(half, 1)
    rate = jnp.pad(jnp.tile(diffusion, 4), (0, LANES - MAIN))[None]
    order = np.arange(half).reshape(16, 5, 4).transpose(2, 1, 0).reshape(1, half).astype(np.int32)

    rows = state.transpose(0, 2, 1, 3).reshape(4, 5, 4, 24, lon_count)
    waves = forward_waves(rows, tables).reshape(15, 128, own_waves, 2, LANES)
    received = exchange_call(to_owner_kernel, waves, (4, 15, own_waves, 32, 2, LANES), 0)
    received = received.reshape(4, 15, own_waves, 64, LANES)
    filtered = spectral_filter(first, received, legendre, weight, rate, order, pick)
    filtered = filtered.reshape(4, 15, own_waves, 32, 2, LANES)
    returned = exchange_call(to_slab_kernel, filtered, (15, 128, own_waves, 2, LANES), 1)
    smoothed = inverse_waves(returned.reshape(15, lon_count, LANES), tables)
    return smoothed.reshape(4, 20, 24, lon_count).transpose(0, 2, 1, 3)


def solution(mesh):
    return jax.shard_map(
        on_device,
        mesh=mesh,
        in_specs=(
            P("traj", None, "grid", None),
            P(),
            P(),
            P(("traj", "grid"), None, None, None),
            P(),
            P(),
        ),
        out_specs=P("traj", None, "grid", None),
        check_vma=False,
    )
```

```python
import functools
import math

import jax
import jax.numpy as jnp
import numpy as np
from jax import lax
from jax.experimental import pallas as pl
from jax.experimental.pallas import tpu as pltpu
from jax.sharding import PartitionSpec as P

MESH = pl.DeviceIdType.MESH
LANES = 128
MAIN = 96
TAIL = 32
BIG = 60 * 2**20


def angle_tables(lon_count):
    points = np.arange(lon_count)
    unit = 2.0 * math.pi / lon_count
    order = (np.arange(5)[:, None] + 80 * np.arange(8)[None, :]).reshape(40)
    coarse = (order[:, None] * points[None, :]) % lon_count * unit
    fine = (5 * np.arange(16)[:, None] * points[None, :]) % lon_count * unit
    fine = (fine[:, None, :] + np.arange(2)[None, :, None] * (math.pi / 2)).reshape(32, lon_count)
    coarse = coarse[:, None, :]
    return [np.asarray(t, np.float32) for t in (np.cos(coarse), np.sin(coarse), np.cos(fine), np.sin(fine))]


def fill_rows(table, base, chunk, angles, scale, halve_first):
    coarse_cos, coarse_sin, fine_cos, fine_sin = angles

    @pl.loop(0, 8)
    def _(a):
        row = chunk * 8 + a
        rows = (coarse_cos[row] * scale) * fine_cos[...] - (coarse_sin[row] * scale) * fine_sin[...]
        if halve_first:
            line = lax.broadcasted_iota(jnp.int32, rows.shape, 0)
            rows = jnp.where(jnp.logical_and(row == 0, line < 2), rows * 0.5, rows)
        table[pl.ds(pl.multiple_of(base + a * 32, 32), 32), :] = rows.astype(table.dtype)


def offsets():
    traj, grid = lax.axis_index("traj"), lax.axis_index("grid")
    core, y = lax.rem(traj, 2), lax.rem(grid, 2) * 2 + lax.div(traj, 2)
    x, z = lax.rem(lax.div(grid, 2), 4), lax.div(grid, 8)
    rows = [lax.rem(y + step, 4) for step in range(4)]
    rows = [(lax.rem(row, 2) * 2, lax.div(row, 2)) for row in rows]

    def partners(group, steps):
        there_core = lax.rem(core + lax.div(group, 16), 2)
        there_z = lax.rem(z + lax.rem(lax.div(group, 4), 4), 4)
        there_x = lax.rem(x + lax.rem(group, 4), 4)
        column = (there_z * 4 + there_x) * 2
        return [(rows[step][0] + there_core, column + rows[step][1]) for step in steps]

    return partners


def for_partners(action):
    partners = offsets()
    for there in partners(0, (1, 2, 3)):
        action(there)

    def group_of(group, carry):
        for there in partners(group, (0, 1, 2, 3)):
            action(there)
        return carry

    lax.fori_loop(1, 32, group_of, 0)


def slab_slot(grid):
    return jnp.where(grid < 16, grid, 47 - grid)


def pair(index):
    return pl.ds(pl.multiple_of(index * 2, 2), 2)


def clone_columns(counts, slot_perm):
    row16 = lax.broadcasted_iota(jnp.int32, (16, 16), 0)
    col16 = lax.broadcasted_iota(jnp.int32, (16, 16), 1)
    copy_end = jnp.sum(jnp.where(col16 <= row16, counts, 0), axis=1, keepdims=True)
    copy_parent = jnp.sum((copy_end <= col16).astype(jnp.int32), axis=0, keepdims=True)
    parents = jnp.sum(jnp.where(slot_perm == row16, copy_parent, 0), axis=1, keepdims=True)

    def labels(shape, axis):
        lane = lax.broadcasted_iota(jnp.int32, shape, axis)
        within = lane % LANES
        return within < MAIN, lane // LANES * 4 + within // 24, within % 24

    valid, slot, field = labels((16, 4 * LANES), 1)
    here = jnp.logical_and(valid, slot == lax.broadcasted_iota(jnp.int32, (16, 4 * LANES), 0))
    wanted = jnp.sum(jnp.where(here, parents * 24 + field + 1, 0), axis=0, keepdims=True)
    valid, member, field = labels((4 * LANES, 4 * LANES), 0)
    return jnp.logical_and(valid, member * 24 + field + 1 == wanted).astype(jnp.bfloat16)


def spectral_chunk(chunk, first, received, legendre, sent, weight, rate, take, pick, split, paired, cloned, woven):
    wave = first + chunk
    lane = lax.broadcasted_iota(jnp.int32, (64, LANES), 1)

    @pl.loop(0, 4)
    def _(g):
        for q in range(5):
            parts = [received[chunk, g, 3 * q + a].astype(jnp.float32) for a in range(3)]
            moved = [pltpu.roll(parts[a], TAIL * (a + 1), 1) for a in range(3)]
            parts.append(jnp.where(lane < TAIL, moved[0], jnp.where(lane < 2 * TAIL, moved[1], moved[2])))
            for i in range(4):
                split[4 * q + i] = parts[i]
        for q in range(5):
            for i in range(4):
                rows = slice(80 * i + 16 * q, 80 * i + 16 * q + 16)
                scale = weight[rows]
                for r in range(2):
                    north = split[4 * q + i, pl.ds(r, 16, stride=2), :]
                    south = split[4 * (4 - q) + 3 - i, pl.ds(32 + r, 16, stride=2), :]
                    paired[0, 4 * r + g, rows] = ((north + south) * scale).astype(jnp.bfloat16)
                    paired[1, 4 * r + g, rows] = ((north - south) * scale).astype(jnp.bfloat16)

    half = legendre.shape[-1]
    returned = []
    for p in range(2):
        table = jnp.dot(legendre[chunk, p], take[...], preferred_element_type=jnp.float32).astype(jnp.bfloat16)
        columns = jnp.concatenate([paired[p, c] for c in range(8)], axis=1)
        spectrum = jnp.dot(table, columns, preferred_element_type=jnp.float32)
        degree = 2 * lax.broadcasted_iota(jnp.int32, (half, LANES), 0) + (wave + p) % 2
        ratio = (degree * (degree + 1)).astype(jnp.float32) / float(2 * half * (2 * half - 1))
        damping = 1.0 / (1.0 + rate[...] * (ratio * ratio))
        keep = degree >= wave
        for r in range(2):
            kept = [
                jnp.where(keep, spectrum[:, LANES * c:LANES * (c + 1)] * damping, 0.0).astype(jnp.bfloat16)
                for c in range(4 * r, 4 * r + 4)
            ]
            cloned[p, :, 512 * r:512 * (r + 1)] = jnp.dot(
                jnp.concatenate(kept, axis=1), pick[...], preferred_element_type=jnp.float32
            ).astype(jnp.bfloat16)
        returned.append(
            lax.dot_general(table, cloned[p], (((0,), (0,)), ((), ())), preferred_element_type=jnp.float32)
        )
    main_lanes = lax.broadcasted_iota(jnp.int32, (80, LANES), 1) < MAIN
    for c in range(8):
        r, g = c // 4, c % 4
        cols = slice(LANES * c, LANES * (c + 1))
        even, odd = returned[0][:, cols], returned[1][:, cols]
        north, south = even + odd, even - odd
        for a in range(3):
            shift = MAIN - TAIL * a
            upper = jnp.where(main_lanes, north[80 * a:80 * a + 80], pltpu.roll(north[240:320], shift, 1))
            lower = jnp.where(main_lanes, south[80 * (3 - a):80 * (3 - a) + 80], pltpu.roll(south[0:80], shift, 1))
            for q in range(5):
                woven[15 * g + 3 * q + a, pl.ds(r, 16, stride=2), :] = upper[16 * q:16 * q + 16]
                woven[15 * g + 3 * q + a, pl.ds(32 + r, 16, stride=2), :] = lower[16 * (4 - q):16 * (4 - q) + 16]
    for g in range(4):
        for tile in range(15):
            sent[chunk, g, tile] = woven[15 * g + tile].astype(jnp.bfloat16)


def step_kernel(x_hbm, leg_hbm, coarse_cos, coarse_sin, fine_cos, fine_sin, counts, slot_perm, quad_weight, diffusion,
                order, z_hbm, table_hbm, x_ref, legendre, rows_ref, table, inverse, waves, received, sent, weight, rate,
                take, pick, split, paired, cloned, woven, x_sem, load_sem, out_send, out_recv, back_send, back_recv):
    angles = (coarse_cos, coarse_sin, fine_cos, fine_sin)
    lon_count = x_hbm.shape[-1]
    traj, grid = lax.axis_index("traj"), lax.axis_index("grid")
    device = traj * 32 + grid
    loads = [pltpu.make_async_copy(x_hbm.at[:, q], x_ref.at[:, q], x_sem.at[q]) for q in range(5)]
    for load in loads:
        load.start()
    leg_load = pltpu.make_async_copy(leg_hbm, legendre, load_sem.at[0])
    leg_load.start()
    barrier = pltpu.get_barrier_semaphore()
    for_partners(lambda there: pl.semaphore_signal(barrier, inc=1, device_id=there, device_id_type=MESH))

    def fourier(chunk, q):
        found = lax.dot_general(
            table[...], rows_ref[q], (((1,), (1,)), ((), ())), preferred_element_type=jnp.float32
        ).astype(jnp.bfloat16)
        for a in range(3):
            waves[chunk, 3 * q + a] = found[:, LANES * a:LANES * (a + 1)]

    def send_out(chunk):
        pltpu.make_async_copy(
            waves.at[chunk, :, pair(device)], received.at[chunk, traj, :, pair(slab_slot(grid))], out_recv.at[chunk]
        ).start()
        for_partners(lambda there: pltpu.make_async_remote_copy(
            waves.at[chunk, :, pair(there[0] * 32 + there[1])],
            received.at[chunk, traj, :, pair(slab_slot(grid))],
            out_send.at[chunk], out_recv.at[chunk], device_id=there, device_id_type=MESH,
        ).start())

    def send_back(chunk):
        pltpu.make_async_copy(
            sent.at[chunk, traj, :, pair(slab_slot(grid))], z_hbm.at[chunk, :, device], back_recv.at[chunk]
        ).start()
        for_partners(lambda there: pltpu.make_async_remote_copy(
            sent.at[chunk, there[0], :, pair(slab_slot(there[1]))], z_hbm.at[chunk, :, device],
            back_send.at[chunk], back_recv.at[chunk], device_id=there, device_id_type=MESH,
        ).start())

    fill_rows(table, 0, 0, angles, 1.0 / lon_count, False)
    for q in range(5):
        loads[q].wait()
        tail = jnp.concatenate([x_ref[t, q, 3].astype(jnp.float32) for t in range(4)], axis=0)
        tiles = []
        for a in range(3):
            tiles += [x_ref[t, q, a].astype(jnp.float32) for t in range(4)]
            tiles.append(tail[TAIL * a:TAIL * (a + 1)])
        rows_ref[q] = jnp.concatenate(tiles, axis=0).astype(jnp.bfloat16)
        fourier(0, q)
    pl.semaphore_wait(barrier, 127)
    send_out(0)

    @pl.loop(1, 5)
    def _(chunk):
        fill_rows(table, 0, chunk, angles, 1.0 / lon_count, False)
        for q in range(5):
            fourier(chunk, q)
        send_out(chunk)

    half = legendre.shape[-1]
    pick[...] = clone_columns(counts[...], slot_perm[...])
    chosen = lax.broadcasted_iota(jnp.int32, (half, half), 0) == order[...]
    take[...] = chosen.astype(jnp.bfloat16)
    row = lax.broadcasted_iota(jnp.int32, (half, half), 0)
    place = row % 16 * 20 + row % 80 // 16 * 4 + row // 80
    at_place = lax.broadcasted_iota(jnp.int32, (half, half), 1) == place
    weight[...] = jnp.sum(jnp.where(at_place, quad_weight[...], 0.0), axis=1, keepdims=True)
    levels = diffusion.shape[-1]
    row, col = (lax.broadcasted_iota(jnp.int32, (levels, levels), axis) for axis in (0, 1))
    per_level = jnp.sum(jnp.where(row == col, diffusion[...], 0.0), axis=1, keepdims=True)
    row, col = (lax.broadcasted_iota(jnp.int32, (levels, LANES), axis) for axis in (0, 1))
    here = jnp.logical_and(col % levels == row, col < MAIN)
    rate[...] = jnp.sum(jnp.where(here, per_level, 0.0), axis=0, keepdims=True)

    @pl.loop(0, 5)
    def _(chunk):
        fill_rows(inverse, chunk * 256, chunk, angles, 2.0, True)

    table_out = pltpu.make_async_copy(inverse, table_hbm, load_sem.at[1])
    table_out.start()
    leg_load.wait()

    @pl.loop(0, 5)
    def _(chunk):
        pltpu.make_async_copy(received.at[chunk], received.at[chunk], out_recv.at[chunk]).wait()
        spectral_chunk(chunk, device * 5, received, legendre, sent, weight, rate, take, pick, split, paired, cloned, woven)
        send_back(chunk)

    table_out.wait()

    @pl.loop(0, 5)
    def _(chunk):
        others = waves.at[chunk, :, pl.ds(0, 254)]
        pltpu.make_async_copy(others, others, out_send.at[chunk]).wait()
        pltpu.make_async_copy(others, others, back_send.at[chunk]).wait()
        pltpu.make_async_copy(z_hbm.at[chunk], z_hbm.at[chunk], back_recv.at[chunk]).wait()


def transform_step(rows, legendre, tables, counts, slot_perm, quad_weight, diffusion, order):
    lon_count = rows.shape[-1]
    chunks, _, half, _ = legendre.shape
    vmem = pl.BlockSpec(memory_space=pltpu.VMEM)
    anywhere = pl.BlockSpec(memory_space=pl.ANY)
    return pl.pallas_call(
        step_kernel,
        out_shape=(
            jax.ShapeDtypeStruct((chunks, 15, 128, 2, LANES), jnp.bfloat16),
            jax.ShapeDtypeStruct((lon_count, lon_count), jnp.bfloat16),
        ),
        in_specs=[anywhere, anywhere] + [vmem] * 9,
        out_specs=(anywhere, anywhere),
        scratch_shapes=[
            pltpu.VMEM(rows.shape, jnp.bfloat16),
            pltpu.VMEM(legendre.shape, jnp.bfloat16),
            pltpu.VMEM((5, 384, lon_count), jnp.bfloat16),
            pltpu.VMEM((256, lon_count), jnp.bfloat16),
            pltpu.VMEM((lon_count, lon_count), jnp.bfloat16),
            pltpu.VMEM((chunks, 15, 256, LANES), jnp.bfloat16),
            pltpu.VMEM((chunks, 4, 15, 64, LANES), jnp.bfloat16),
            pltpu.VMEM((chunks, 4, 15, 64, LANES), jnp.bfloat16),
            pltpu.VMEM((half, 1), jnp.float32),
            pltpu.VMEM((1, LANES), jnp.float32),
            pltpu.VMEM((half, half), jnp.bfloat16),
            pltpu.VMEM((4 * LANES, 4 * LANES), jnp.bfloat16),
            pltpu.VMEM((20, 64, LANES), jnp.float32),
            pltpu.VMEM((2, 8, half, LANES), jnp.bfloat16),
            pltpu.VMEM((2, half, 8 * LANES), jnp.bfloat16),
            pltpu.VMEM((60, 64, LANES), jnp.float32),
            pltpu.SemaphoreType.DMA((5,)),
            pltpu.SemaphoreType.DMA((2,)),
            pltpu.SemaphoreType.DMA((5,)),
            pltpu.SemaphoreType.DMA((5,)),
            pltpu.SemaphoreType.DMA((5,)),
            pltpu.SemaphoreType.DMA((5,)),
        ],
        compiler_params=pltpu.CompilerParams(collective_id=0, has_side_effects=True, vmem_limit_bytes=BIG),
    )(rows, legendre, *tables, counts, slot_perm, quad_weight, diffusion, order)


def inverse_kernel(z_ref, table, x_ref):
    depth = table.shape[0]
    waves = jnp.concatenate([z_ref[:, a].reshape(depth, LANES) for a in range(3)], axis=1)
    rows = lax.dot_general(waves, table[...], (((0,), (0,)), ((), ())), preferred_element_type=jnp.float32)
    for a in range(3):
        for t in range(4):
            base = LANES * a + 24 * t
            x_ref[t, 0, a] = rows[base:base + 24].astype(jnp.bfloat16)
    tail = jnp.concatenate([rows[LANES * a + MAIN:LANES * (a + 1)] for a in range(3)], axis=0)
    for t in range(4):
        x_ref[t, 0, 3] = tail[24 * t:24 * t + 24].astype(jnp.bfloat16)


def inverse_waves(waves, table):
    lon_count = table.shape[1]
    return pl.pallas_call(
        inverse_kernel,
        grid=(5,),
        out_shape=jax.ShapeDtypeStruct((4, 5, 4, 24, lon_count), jnp.bfloat16),
        in_specs=[
            pl.BlockSpec((5, 3, 256, LANES), lambda q: (0, q, 0, 0)),
            pl.BlockSpec(table.shape, lambda q: (0, 0)),
        ],
        out_specs=pl.BlockSpec((4, 1, 4, 24, lon_count), lambda q: (0, q, 0, 0, 0)),
        compiler_params=pltpu.CompilerParams(vmem_limit_bytes=BIG),
    )(waves, table)


def on_device(state, counts, slot_perm, legendre, quad_weight, diffusion):
    lon_count = state.shape[-1]
    chunks, _, half, _ = legendre.shape
    order = np.arange(half).reshape(16, 5, 4).transpose(2, 1, 0).reshape(1, half).astype(np.int32)
    rows = state.transpose(0, 2, 1, 3).reshape(4, 5, 4, 24, lon_count)
    returned, table = transform_step(
        rows, legendre, angle_tables(lon_count), counts[None], slot_perm[None], quad_weight[None], diffusion[None], order
    )
    smoothed = inverse_waves(returned.reshape(chunks, 15, 256, LANES), table)
    return smoothed.reshape(4, 20, 24, lon_count).transpose(0, 2, 1, 3)


def solution(mesh):
    return jax.shard_map(
        on_device,
        mesh=mesh,
        in_specs=(
            P("traj", None, "grid", None),
            P(),
            P(),
            P(("traj", "grid"), None, None, None),
            P(),
            P(),
        ),
        out_specs=P("traj", None, "grid", None),
        check_vma=False,
    )
```
